32 devices in a mesh: tm: 8 (over z, x), rows: 4 (over y, core).
Axes of the slice: x: 2, y: 2, z: 4, core: 2. Of those that a mesh axis runs over, the one named last changes fastest.
Arguments:
- slc_stack: bfloat16 [32, 2, 32, 2048], P('tm', None, 'rows'), may hold values from -6 to 6
- partner_count: int32 [32], P('tm'), may hold values from 2 to 6, as said below
- look_sizes: int32 [32, 2], P('tm'), may hold values from 1 to 8, as said below
Outputs:
- interferogram: bfloat16 [32, 6, 2, 32, 2048], P('tm', None, None, 'rows')
- coherence: bfloat16 [32, 6, 32, 2048], P('tm', None, 'rows')
The draws below stay inside these ranges and needn't reach their ends.
Inputs may be any that keep to these rules, and one draw needn't show every extreme that they name: `partner_count`: some acquisition has 6 partners and some has 2. `look_sizes`: Half-heights run from 1 to 2, half-widths from 2 to 8; some acquisition has (2, 8) and some (1, 2).
All inputs are finite; a program needn't handle non-finite values.
Results may differ from the reference program's by a relative error of at most 0.0049.
Values may be sent and summed in bfloat16 or wider, within the bound.
A program may use at most 64 MiB of HBM per device.

```python
import jax
import jax.numpy as jnp
from jax import lax

MAXP = 6
HR = 2
HC = 8
COLS = 2048
ACQ = 32
IMG_ROWS = 32


def draw_partner_count(key, part):
    key_counts = jax.random.fold_in(key, 11)
    key_top = jax.random.fold_in(key, 12)
    key_low = jax.random.fold_in(key, 13)
    counts = jax.random.randint(key_counts, (ACQ,), 2, MAXP + 1)
    top_at = jax.random.randint(key_top, (), 0, ACQ)
    low_at = (top_at + 1 + jax.random.randint(key_low, (), 0, ACQ - 1)) % ACQ
    counts = counts.at[top_at].set(MAXP).at[low_at].set(2)
    return counts.astype(jnp.int32)


def draw_look_sizes(key, part):
    key_rows = jax.random.fold_in(key, 21)
    key_cols = jax.random.fold_in(key, 22)
    key_top = jax.random.fold_in(key, 23)
    key_low = jax.random.fold_in(key, 24)
    half_rows = jax.random.randint(key_rows, (ACQ,), 1, HR + 1)
    half_cols = jax.random.randint(key_cols, (ACQ,), 2, HC + 1)
    top_at = jax.random.randint(key_top, (), 0, ACQ)
    low_at = (top_at + 1 + jax.random.randint(key_low, (), 0, ACQ - 1)) % ACQ
    half_rows = half_rows.at[top_at].set(HR).at[low_at].set(1)
    half_cols = half_cols.at[top_at].set(HC).at[low_at].set(2)
    return jnp.stack([half_rows, half_cols], 1).astype(jnp.int32)


def levels(own_key, extent, split, least, top_value):
    loudness, own = 1.0, jax.random.fold_in(own_key, 6)
    for axis_at, blocks in split:
        heights = jnp.exp(jax.random.uniform(jax.random.fold_in(own, axis_at), (blocks,), jnp.float32, least / len(split), top_value / len(split)))
        loudness = loudness * jnp.repeat(heights, extent[axis_at] // blocks).reshape([-1 if axis == axis_at else 1 for axis in range(len(extent))])
    return loudness


def normal_values(stream_key, shape, width, reach, split=(), kind=jnp.bfloat16):
    array = width * jax.random.normal(stream_key, shape, jnp.float32)
    if split:
        array = array * levels(stream_key, shape, split, -0.22, 0.18)
    return jnp.clip(array, -reach, reach).astype(kind)


def setup_inputs(seed: int = 0) -> dict:
    key_of = jax.random.split(jax.random.key(seed), 4)
    return {
        "slc_stack": normal_values(key_of[0], (ACQ, 2, IMG_ROWS, COLS), 1.0, 6.0, ((0, 8), (2, 4))),
        "partner_count": draw_partner_count(jax.random.fold_in(key_of[3], 71), 0),
        "look_sizes": draw_look_sizes(jax.random.fold_in(key_of[3], 71), 0),
    }


epsilon = 1e-06

def window_rows(fields, half_rows):
    row_count = fields.shape[-2]
    padded = jnp.pad(fields, [(0, 0)] * (fields.ndim - 2) + [(HR, HR), (0, 0)])
    total = jnp.zeros(fields.shape, jnp.float32)
    for offset in range(-HR, HR + 1):
        piece = padded[..., HR + offset:HR + offset + row_count, :]
        total = total + jnp.where(abs(offset) <= half_rows, piece, 0.0)
    return total

def window_cols(summed, half_cols):
    col_count = summed.shape[-1]
    padded = jnp.pad(summed.astype(jnp.float32), [(0, 0)] * (summed.ndim - 1) + [(HC, HC)])
    total = jnp.zeros(summed.shape, jnp.float32)
    for offset in range(-HC, HC + 1):
        piece = padded[..., HC + offset:HC + offset + col_count]
        total = total + jnp.where(abs(offset) <= half_cols, piece, 0.0)
    return total

def reference(slc_stack, partner_count, look_sizes):
    acq_total = slc_stack.shape[0]

    def one_acquisition(acq_index):
        own = lax.dynamic_index_in_dim(slc_stack, acq_index, 0, keepdims=False).astype(jnp.float32)
        half_rows = look_sizes[acq_index, 0]
        half_cols = look_sizes[acq_index, 1]
        own_power = own[0] * own[0] + own[1] * own[1]
        boxed_own = window_cols(window_rows(own_power, half_rows).astype(jnp.bfloat16), half_cols)
        offsets = jnp.arange(1, MAXP + 1, dtype=jnp.int32)
        partner_index = jnp.minimum(acq_index + offsets, acq_total - 1).astype(jnp.int32)
        partners = slc_stack[partner_index].astype(jnp.float32)
        real_part = own[0] * partners[:, 0] + own[1] * partners[:, 1]
        imag_part = own[1] * partners[:, 0] - own[0] * partners[:, 1]
        power = partners[:, 0] * partners[:, 0] + partners[:, 1] * partners[:, 1]
        terms = jnp.stack([real_part, imag_part, power], 1)
        boxed = window_cols(window_rows(terms, half_rows).astype(jnp.bfloat16), half_cols)
        live = (offsets <= partner_count[acq_index]) & (acq_index + offsets < acq_total)
        area = ((2 * half_rows + 1) * (2 * half_cols + 1)).astype(jnp.float32)
        ifg = jnp.where(live[:, None, None, None], boxed[:, :2] / area, 0.0).astype(jnp.bfloat16)
        magnitude = jnp.sqrt(boxed[:, 0] * boxed[:, 0] + boxed[:, 1] * boxed[:, 1])
        coh = magnitude * lax.rsqrt(boxed_own[None] * boxed[:, 2] + epsilon)
        coh = jnp.where(live[:, None, None], coh, 0.0).astype(jnp.bfloat16)
        return (ifg, coh)
    interferogram, coherence = lax.map(one_acquisition, jnp.arange(acq_total, dtype=jnp.int32))
    return (interferogram, coherence)
```

```python
import functools

import jax
import jax.numpy as jnp
from jax import lax
from jax.experimental import pallas as pl
from jax.experimental.pallas import tpu as pltpu
from jax.sharding import PartitionSpec as P

MAXP = 6
HR = 2
LANES = 128
BLOCK = 256

epsilon = 1e-06


def extended_2(block, sides, width):
    for axis, dim in sides:
        count = lax.axis_size(axis)
        forward = [(i, i + 1) for i in range(count - 1)]
        backward = [(target, source) for source, target in forward]
        low = lax.ppermute(
            lax.slice_in_dim(block, block.shape[dim] - width, None, axis=dim), axis, forward
        )
        high = lax.ppermute(lax.slice_in_dim(block, 0, width, axis=dim), axis, backward)
        block = jnp.concatenate([low, block, high], axis=dim)
    return block


def passed_along(block, axis, distance):
    devices = range(lax.axis_size(axis))
    route = [(i - distance, i) for i in devices if i - distance in devices]
    return lax.ppermute(block, axis, route)


def compute_kernel(
    acq_total, counts, looks, src, ifg, coh, planes, power, sums, wide, boxed, stage
):
    acq = pl.program_id(0)
    total, _, ext_rows, cols = src.shape
    per_dev = total - MAXP
    rows = ext_rows - 2 * HR
    tiles = cols // LANES
    blocks = cols // BLOCK
    fields = 3 * MAXP + 1

    @pl.when(acq == 0)
    def _():
        @pl.loop(0, total)
        def _(p):
            for part in range(2):
                for t in range(tiles):
                    piece = src[p, part, :, t * LANES : (t + 1) * LANES].astype(jnp.float32)
                    stage[part, t * 16 : t * 16 + ext_rows, :] = piece
            for r in range(ext_rows):
                real = stage[0, pl.ds(r, tiles, stride=16), :]
                imag = stage[1, pl.ds(r, tiles, stride=16), :]
                planes[p, 0, r] = real
                planes[p, 1, r] = imag
                power[p, r] = real * real + imag * imag

        zero = jnp.zeros((wide.shape[1], LANES), wide.dtype)
        wide[0, :, :LANES] = zero
        wide[blocks, :, LANES:] = zero

    half_rows = looks[acq, 0]
    half_cols = looks[acq, 1]
    outer = jnp.where(half_rows >= HR, 1.0, 0.0).astype(jnp.float32)

    def row_window(get, field):
        for h in range(0, tiles, 8):
            x = get(h)
            pairs = [x[r] + x[r + 1] for r in range(1, rows + 2)]
            for r in range(rows):
                inner = pairs[r] + x[r + 3]
                edge = (x[r] + x[r + 4]) * outer
                sums[field, pl.ds(h * rows + r, 8, stride=rows), :] = inner + edge

    def row(p, part, r, h):
        return planes[p, part, r, h : h + 8, :]

    def own_power(h):
        return [power[acq, r, h : h + 8, :] for r in range(ext_rows)]

    row_window(own_power, 3 * MAXP)

    @pl.loop(0, MAXP)
    def _(j):
        p = acq + j + 1

        def real_part(h):
            return [
                row(acq, 0, r, h) * row(p, 0, r, h) + row(acq, 1, r, h) * row(p, 1, r, h)
                for r in range(ext_rows)
            ]

        def imag_part(h):
            return [
                row(acq, 1, r, h) * row(p, 0, r, h) - row(acq, 0, r, h) * row(p, 1, r, h)
                for r in range(ext_rows)
            ]

        def partner_power(h):
            return [power[p, r, h : h + 8, :] for r in range(ext_rows)]

        row_window(real_part, 3 * j)
        row_window(imag_part, 3 * j + 1)
        row_window(partner_power, 3 * j + 2)

    @pl.loop(0, (fields + 1) // 2)
    def _(f):
        for t in range(tiles):
            both = jnp.concatenate(
                [
                    sums[2 * f, t * rows : (t + 1) * rows, :],
                    sums[2 * f + 1, t * rows : (t + 1) * rows, :],
                ],
                0,
            ).astype(jnp.bfloat16)
            m, side = (t + 1) // 2, (t + 1) % 2
            wide[m, pl.ds(pl.multiple_of(f * 16, 16), 16), side * LANES : (side + 1) * LANES] = both

    inner = lax.broadcasted_iota(jnp.int32, (BLOCK, BLOCK), 0)
    place = lax.broadcasted_iota(jnp.int32, (BLOCK, BLOCK), 1)
    lead = jnp.where(jnp.abs(inner - LANES - place) <= half_cols, 1.0, 0.0).astype(jnp.bfloat16)
    tail = jnp.where(jnp.abs(inner + LANES - place) <= half_cols, 1.0, 0.0).astype(jnp.bfloat16)
    depth = wide.shape[1]
    boxed[...] = (
        jnp.dot(
            wide[0:blocks].reshape(blocks * depth, BLOCK), lead, preferred_element_type=jnp.float32
        )
        + jnp.dot(
            wide[1 : blocks + 1].reshape(blocks * depth, BLOCK),
            tail,
            preferred_element_type=jnp.float32,
        )
    ).reshape(blocks, depth, BLOCK)

    area = ((2 * half_rows + 1) * (2 * half_cols + 1)).astype(jnp.float32)
    scale = 1.0 / jnp.full((rows, BLOCK), area, jnp.float32)
    index = lax.axis_index("tm") * per_dev + acq
    count = counts[acq]

    @pl.loop(0, blocks)
    def _(n):
        own = boxed[n, 3 * MAXP * rows : (3 * MAXP + 1) * rows, :]
        where = pl.ds(pl.multiple_of(n * BLOCK, BLOCK), BLOCK)
        for j in range(MAXP):
            live = (j < count) & (index + j + 1 < acq_total)
            real = boxed[n, (3 * j) * rows : (3 * j + 1) * rows, :]
            imag = boxed[n, (3 * j + 1) * rows : (3 * j + 2) * rows, :]
            other = boxed[n, (3 * j + 2) * rows : (3 * j + 3) * rows, :]
            magnitude = jnp.sqrt(real * real + imag * imag)
            value = magnitude * lax.rsqrt(own * other + epsilon)
            ifg[0, j, 0, :, where] = jnp.where(live, real * scale, 0.0).astype(ifg.dtype)
            ifg[0, j, 1, :, where] = jnp.where(live, imag * scale, 0.0).astype(ifg.dtype)
            coh[0, j, :, where] = jnp.where(live, value, 0.0).astype(coh.dtype)


def computed(extended, partner_count, look_sizes, acq_total):
    total, _, ext_rows, cols = extended.shape
    per_dev, rows = total - MAXP, ext_rows - 2 * HR
    tiles, blocks = cols // LANES, cols // BLOCK
    fields = 3 * MAXP + 2
    return pl.pallas_call(
        functools.partial(compute_kernel, acq_total),
        grid=(per_dev,),
        in_specs=[
            pl.BlockSpec(memory_space=pltpu.SMEM),
            pl.BlockSpec(memory_space=pltpu.SMEM),
            pl.BlockSpec(extended.shape, lambda a: (0, 0, 0, 0)),
        ],
        out_specs=[
            pl.BlockSpec((1, MAXP, 2, rows, cols), lambda a: (a, 0, 0, 0, 0)),
            pl.BlockSpec((1, MAXP, rows, cols), lambda a: (a, 0, 0, 0)),
        ],
        out_shape=[
            jax.ShapeDtypeStruct((per_dev, MAXP, 2, rows, cols), jnp.bfloat16),
            jax.ShapeDtypeStruct((per_dev, MAXP, rows, cols), jnp.bfloat16),
        ],
        scratch_shapes=[
            pltpu.VMEM((total, 2, ext_rows, tiles, LANES), jnp.float32),
            pltpu.VMEM((total, ext_rows, tiles, LANES), jnp.float32),
            pltpu.VMEM((fields, tiles * rows, LANES), jnp.float32),
            pltpu.VMEM((blocks + 1, fields * rows, BLOCK), jnp.bfloat16),
            pltpu.VMEM((blocks, fields * rows, BLOCK), jnp.float32),
            pltpu.VMEM((2, tiles * 16, LANES), jnp.float32),
        ],
        compiler_params=pltpu.CompilerParams(vmem_limit_bytes=48 * 1024 * 1024),
        name="insar_boxes",
    )(partner_count, look_sizes, extended)


def local(slc_stack, partner_count, look_sizes):
    per_dev = slc_stack.shape[0]
    haloed = extended_2(slc_stack, (("rows", 2),), HR)
    nearby = passed_along(haloed, "tm", -1)
    farther = passed_along(haloed[: MAXP - per_dev], "tm", -2)
    extended = jnp.concatenate([haloed, nearby, farther], 0)
    acq_total = lax.axis_size("tm") * per_dev
    return tuple(computed(extended, partner_count, look_sizes, acq_total))


def solution(mesh):
    return jax.shard_map(
        local,
        mesh=mesh,
        in_specs=(P("tm", None, "rows", None), P("tm"), P("tm", None)),
        out_specs=(P("tm", None, None, "rows", None), P("tm", None, "rows", None)),
        check_vma=False,
    )
```

```python
import functools

import jax
import jax.numpy as jnp
from jax import lax
from jax.experimental import pallas as pl
from jax.experimental.pallas import tpu as pltpu
from jax.sharding import PartitionSpec as P

MAXP = 6
HR = 2
LANES = 128
BLOCK = 256

epsilon = 1e-06
MESH = pl.DeviceIdType.MESH


def gather_kernel(x, held, send_sem, recv_sem):
    tm, line = lax.axis_index("tm"), lax.axis_index("rows")
    tm_count, line_count = lax.axis_size("tm"), lax.axis_size("rows")
    per_dev, _, rows = x.shape[:3]
    total = held.shape[0]
    far = MAXP - per_dev
    even = lax.rem(tm, 2) == 0
    odd = lax.rem(tm, 2) == 1
    steps = [
        (tm >= 1, {"tm": tm - 1}),
        (tm >= 2, {"tm": tm - 2}),
        (tm + 1 < tm_count, {"tm": tm + 1}),
        (tm + 2 < tm_count, {"tm": tm + 2}),
        (line >= 1, {"rows": line - 1}),
        (line + 1 < line_count, {"rows": line + 1}),
    ]
    barrier = pltpu.get_barrier_semaphore()
    for there, device in steps:

        @pl.when(there)
        def _():
            pl.semaphore_signal(barrier, inc=1, device_id=device, device_id_type=MESH)

    pl.semaphore_wait(barrier, sum(jnp.where(there, 1, 0) for there, _ in steps))

    body = pl.ds(HR, rows)
    forward_slot = 3 * total
    own_slot = 3 * total + far

    def copy(src, dst, send, recv, device):
        return pltpu.make_async_remote_copy(
            src_ref=src,
            dst_ref=dst,
            send_sem=send_sem.at[send],
            recv_sem=recv_sem.at[recv],
            device_id=device,
            device_id_type=MESH,
        )

    def near(k):
        spot = per_dev + k
        return copy(x.at[k], held.at[spot, :, body], spot, spot, {"tm": tm - 1})

    def distant(k):
        spot = 2 * per_dev + k
        return copy(x.at[k], held.at[spot, :, body], spot, spot, {"tm": tm - 2})

    def onward(k):
        spot = per_dev + k
        src = held.at[2 * per_dev + k, :, body]
        return copy(src, held.at[spot, :, body], forward_slot + k, spot, {"tm": tm + 1})

    def down(p):
        src = held.at[p, :, pl.ds(rows, HR)]
        slot = total + p
        return copy(src, held.at[p, :, pl.ds(0, HR)], slot, slot, {"rows": line + 1})

    def up(p):
        src = held.at[p, :, pl.ds(HR, HR)]
        slot = 2 * total + p
        return copy(src, held.at[p, :, pl.ds(HR + rows, HR)], slot, slot, {"rows": line - 1})

    def own_down():
        src = x.at[:, :, pl.ds(rows - HR, HR)]
        dst = held.at[pl.ds(0, per_dev), :, pl.ds(0, HR)]
        return copy(src, dst, own_slot, own_slot, {"rows": line + 1})

    def own_up():
        src = x.at[:, :, pl.ds(0, HR)]
        dst = held.at[pl.ds(0, per_dev), :, pl.ds(HR + rows, HR)]
        return copy(src, dst, own_slot + 1, own_slot + 1, {"rows": line - 1})

    def has(p):
        return tm + p // per_dev < tm_count

    def spread(p):
        @pl.when(has(p) & (line + 1 < line_count))
        def _():
            down(p).start()

        @pl.when(has(p) & (line >= 1))
        def _():
            up(p).start()

    def sends_near(k):
        return (tm >= 1) & (odd if k < far else (tm >= 0))

    for k in range(far):

        @pl.when(tm >= 2)
        def _():
            distant(k).start()

    for k in range(per_dev):

        @pl.when(sends_near(k))
        def _():
            near(k).start()

    @pl.when(line + 1 < line_count)
    def _():
        own_down().start()

    @pl.when(line >= 1)
    def _():
        own_up().start()

    for k in range(far):
        p = 2 * per_dev + k

        @pl.when(has(p))
        def _():
            distant(k).wait_recv()

        @pl.when(has(p) & even)
        def _():
            onward(k).start()

        spread(p)

    for k in list(range(far, per_dev)) + list(range(far)):
        p = per_dev + k

        @pl.when(has(p))
        def _():
            near(k).wait_recv()

        spread(p)

    @pl.when(line >= 1)
    def _():
        own_down().wait_recv()
        own_up().wait_send()

    @pl.when(line + 1 < line_count)
    def _():
        own_up().wait_recv()
        own_down().wait_send()

    for p in range(per_dev, total):

        @pl.when(has(p) & (line + 1 < line_count))
        def _():
            up(p).wait_recv()
            down(p).wait_send()

        @pl.when(has(p) & (line >= 1))
        def _():
            down(p).wait_recv()
            up(p).wait_send()

    for k in range(far):

        @pl.when(tm >= 2)
        def _():
            distant(k).wait_send()

        @pl.when(has(2 * per_dev + k) & even)
        def _():
            onward(k).wait_send()

    for k in range(per_dev):

        @pl.when(sends_near(k))
        def _():
            near(k).wait_send()


def gathered(x):
    per_dev, parts, rows, tiles, lanes = x.shape
    total = per_dev + MAXP
    slots = 3 * total + MAXP
    return pl.pallas_call(
        gather_kernel,
        in_specs=[pl.BlockSpec(memory_space=pl.ANY)],
        out_specs=pl.BlockSpec(memory_space=pl.ANY),
        out_shape=jax.ShapeDtypeStruct((total, parts, rows + 2 * HR, tiles, lanes), x.dtype),
        scratch_shapes=[pltpu.SemaphoreType.DMA((slots,)), pltpu.SemaphoreType.DMA((slots,))],
        compiler_params=pltpu.CompilerParams(collective_id=0, has_side_effects=True),
        name="gather_acquisitions",
    )(x)


def compute_kernel(
    acq_total, counts, looks, own_src, src, ifg, coh, planes, power, sums, wide, boxed
):
    acq = pl.program_id(0)
    total, _, ext_rows, tiles, _ = src.shape
    per_dev = total - MAXP
    rows = ext_rows - 2 * HR
    blocks = tiles * LANES // BLOCK
    fields = 3 * MAXP + 1

    @pl.when(acq == 0)
    def _():
        line = lax.axis_index("rows")
        edge_low, edge_high = line == 0, line == lax.axis_size("rows") - 1

        def place(p, r, parts):
            outside = edge_low if r < HR else edge_high if r >= HR + rows else None
            if outside is not None:
                parts = [jnp.where(outside, 0.0, part) for part in parts]
            planes[p, 0, r] = parts[0]
            planes[p, 1, r] = parts[1]
            power[p, r] = parts[0] * parts[0] + parts[1] * parts[1]

        @pl.loop(0, per_dev)
        def _(p):
            for r in range(ext_rows):
                inside = HR <= r < HR + rows
                ref, at = (own_src, r - HR) if inside else (src, r)
                place(p, r, [ref[p, part, at].astype(jnp.float32) for part in range(2)])

        @pl.loop(per_dev, total)
        def _(p):
            for r in range(ext_rows):
                place(p, r, [src[p, part, r].astype(jnp.float32) for part in range(2)])

        zero = jnp.zeros((wide.shape[1], LANES), wide.dtype)
        wide[0, :, :LANES] = zero
        wide[blocks, :, LANES:] = zero

    half_rows = looks[acq, 0]
    half_cols = looks[acq, 1]
    outer = jnp.where(half_rows >= HR, 1.0, 0.0).astype(jnp.float32)

    def row_window(get, field):
        for h in range(0, tiles, 8):
            x = get(h)
            pairs = [x[r] + x[r + 1] for r in range(1, rows + 2)]
            for r in range(rows):
                inner = pairs[r] + x[r + 3]
                edge = (x[r] + x[r + 4]) * outer
                sums[field, pl.ds(h * rows + r, 8, stride=rows), :] = inner + edge

    def row(p, part, r, h):
        return planes[p, part, r, h : h + 8, :]

    def own_power(h):
        return [power[acq, r, h : h + 8, :] for r in range(ext_rows)]

    row_window(own_power, 3 * MAXP)

    @pl.loop(0, MAXP)
    def _(j):
        p = acq + j + 1

        def real_part(h):
            return [
                row(acq, 0, r, h) * row(p, 0, r, h) + row(acq, 1, r, h) * row(p, 1, r, h)
                for r in range(ext_rows)
            ]

        def imag_part(h):
            return [
                row(acq, 1, r, h) * row(p, 0, r, h) - row(acq, 0, r, h) * row(p, 1, r, h)
                for r in range(ext_rows)
            ]

        def partner_power(h):
            return [power[p, r, h : h + 8, :] for r in range(ext_rows)]

        row_window(real_part, 3 * j)
        row_window(imag_part, 3 * j + 1)
        row_window(partner_power, 3 * j + 2)

    @pl.loop(0, (fields + 1) // 2)
    def _(f):
        for t in range(tiles):
            both = jnp.concatenate(
                [
                    sums[2 * f, t * rows : (t + 1) * rows, :],
                    sums[2 * f + 1, t * rows : (t + 1) * rows, :],
                ],
                0,
            ).astype(jnp.bfloat16)
            m, side = (t + 1) // 2, (t + 1) % 2
            wide[m, pl.ds(pl.multiple_of(f * 16, 16), 16), side * LANES : (side + 1) * LANES] = both

    inner = lax.broadcasted_iota(jnp.int32, (BLOCK, BLOCK), 0)
    place = lax.broadcasted_iota(jnp.int32, (BLOCK, BLOCK), 1)
    lead = jnp.where(jnp.abs(inner - LANES - place) <= half_cols, 1.0, 0.0).astype(jnp.bfloat16)
    tail = jnp.where(jnp.abs(inner + LANES - place) <= half_cols, 1.0, 0.0).astype(jnp.bfloat16)
    depth = wide.shape[1]
    boxed[...] = (
        jnp.dot(
            wide[0:blocks].reshape(blocks * depth, BLOCK), lead, preferred_element_type=jnp.float32
        )
        + jnp.dot(
            wide[1 : blocks + 1].reshape(blocks * depth, BLOCK),
            tail,
            preferred_element_type=jnp.float32,
        )
    ).reshape(blocks, depth, BLOCK)

    area = ((2 * half_rows + 1) * (2 * half_cols + 1)).astype(jnp.float32)
    scale = 1.0 / jnp.full((rows, BLOCK), area, jnp.float32)
    index = lax.axis_index("tm") * per_dev + acq
    count = counts[acq]

    @pl.loop(0, blocks)
    def _(n):
        own = boxed[n, 3 * MAXP * rows : (3 * MAXP + 1) * rows, :]
        where = pl.ds(pl.multiple_of(n * BLOCK, BLOCK), BLOCK)
        for j in range(MAXP):
            live = (j < count) & (index + j + 1 < acq_total)
            real = boxed[n, (3 * j) * rows : (3 * j + 1) * rows, :]
            imag = boxed[n, (3 * j + 1) * rows : (3 * j + 2) * rows, :]
            other = boxed[n, (3 * j + 2) * rows : (3 * j + 3) * rows, :]
            magnitude = jnp.sqrt(real * real + imag * imag)
            value = magnitude * lax.rsqrt(own * other + epsilon)
            ifg[0, j, 0, :, where] = jnp.where(live, real * scale, 0.0).astype(ifg.dtype)
            ifg[0, j, 1, :, where] = jnp.where(live, imag * scale, 0.0).astype(ifg.dtype)
            coh[0, j, :, where] = jnp.where(live, value, 0.0).astype(coh.dtype)


def computed(own, extended, partner_count, look_sizes, acq_total):
    total, _, ext_rows, tiles, _ = extended.shape
    per_dev, rows = total - MAXP, ext_rows - 2 * HR
    cols = tiles * LANES
    blocks = cols // BLOCK
    fields = 3 * MAXP + 2
    return pl.pallas_call(
        functools.partial(compute_kernel, acq_total),
        grid=(per_dev,),
        in_specs=[
            pl.BlockSpec(memory_space=pltpu.SMEM),
            pl.BlockSpec(memory_space=pltpu.SMEM),
            pl.BlockSpec(own.shape, lambda a: (0, 0, 0, 0, 0)),
            pl.BlockSpec(extended.shape, lambda a: (0, 0, 0, 0, 0)),
        ],
        out_specs=[
            pl.BlockSpec((1, MAXP, 2, rows, cols), lambda a: (a, 0, 0, 0, 0)),
            pl.BlockSpec((1, MAXP, rows, cols), lambda a: (a, 0, 0, 0)),
        ],
        out_shape=[
            jax.ShapeDtypeStruct((per_dev, MAXP, 2, rows, cols), jnp.bfloat16),
            jax.ShapeDtypeStruct((per_dev, MAXP, rows, cols), jnp.bfloat16),
        ],
        scratch_shapes=[
            pltpu.VMEM((total, 2, ext_rows, tiles, LANES), jnp.float32),
            pltpu.VMEM((total, ext_rows, tiles, LANES), jnp.float32),
            pltpu.VMEM((fields, tiles * rows, LANES), jnp.float32),
            pltpu.VMEM((blocks + 1, fields * rows, BLOCK), jnp.bfloat16),
            pltpu.VMEM((blocks, fields * rows, BLOCK), jnp.float32),
        ],
        compiler_params=pltpu.CompilerParams(vmem_limit_bytes=48 * 1024 * 1024),
        name="insar_boxes",
    )(partner_count, look_sizes, own, extended)


def local(slc_stack, partner_count, look_sizes):
    per_dev = slc_stack.shape[0]
    tiled = slc_stack.reshape(slc_stack.shape[:-1] + (-1, LANES))
    extended = gathered(tiled)
    acq_total = lax.axis_size("tm") * per_dev
    return tuple(computed(tiled, extended, partner_count, look_sizes, acq_total))


def solution(mesh):
    return jax.shard_map(
        local,
        mesh=mesh,
        in_specs=(P("tm", None, "rows", None), P("tm"), P("tm", None)),
        out_specs=(P("tm", None, None, "rows", None), P("tm", None, "rows", None)),
        check_vma=False,
    )
```

```python
import functools

import jax
import jax.numpy as jnp
from jax import lax
from jax.experimental import pallas as pl
from jax.experimental.pallas import tpu as pltpu
from jax.sharding import PartitionSpec as P

MAXP = 6
HR = 2
LANES = 128
BLOCK = 256

epsilon = 1e-06
MESH = pl.DeviceIdType.MESH


def kernel(
    acq_total, counts, looks, x, ifg, coh,
    held, planes, power, sums, wide, bands, own_box, send_sem, recv_sem,
):
    tm, line = lax.axis_index("tm"), lax.axis_index("rows")
    tm_count, line_count = lax.axis_size("tm"), lax.axis_size("rows")
    per_dev, _, rows = x.shape[:3]
    total = held.shape[0]
    far = MAXP - per_dev
    even = lax.rem(tm, 2) == 0
    odd = lax.rem(tm, 2) == 1
    steps = [
        (tm >= 1, {"tm": tm - 1}),
        (tm >= 2, {"tm": tm - 2}),
        (tm + 1 < tm_count, {"tm": tm + 1}),
        (tm + 2 < tm_count, {"tm": tm + 2}),
        (line >= 1, {"rows": line - 1}),
        (line + 1 < line_count, {"rows": line + 1}),
    ]
    barrier = pltpu.get_barrier_semaphore()
    for there, device in steps:

        @pl.when(there)
        def _():
            pl.semaphore_signal(barrier, inc=1, device_id=device, device_id_type=MESH)

    pl.semaphore_wait(barrier, sum(jnp.where(there, 1, 0) for there, _ in steps))

    body = pl.ds(HR, rows)
    forward_slot = 3 * total
    own_slot = 3 * total + far

    def copy(src, dst, send, recv, device):
        return pltpu.make_async_remote_copy(
            src_ref=src,
            dst_ref=dst,
            send_sem=send_sem.at[send],
            recv_sem=recv_sem.at[recv],
            device_id=device,
            device_id_type=MESH,
        )

    def near(k):
        spot = per_dev + k
        return copy(x.at[k], held.at[spot, :, body], spot, spot, {"tm": tm - 1})

    def distant(k):
        spot = 2 * per_dev + k
        return copy(x.at[k], held.at[spot, :, body], spot, spot, {"tm": tm - 2})

    def onward(k):
        spot = per_dev + k
        src = held.at[2 * per_dev + k, :, body]
        return copy(src, held.at[spot, :, body], forward_slot + k, spot, {"tm": tm + 1})

    def down(p):
        src = held.at[p, :, pl.ds(rows, HR)]
        slot = total + p
        return copy(src, held.at[p, :, pl.ds(0, HR)], slot, slot, {"rows": line + 1})

    def up(p):
        src = held.at[p, :, pl.ds(HR, HR)]
        slot = 2 * total + p
        return copy(src, held.at[p, :, pl.ds(HR + rows, HR)], slot, slot, {"rows": line - 1})

    def own_down():
        src = x.at[:, :, pl.ds(rows - HR, HR)]
        dst = held.at[pl.ds(0, per_dev), :, pl.ds(0, HR)]
        return copy(src, dst, own_slot, own_slot, {"rows": line + 1})

    def own_up():
        src = x.at[:, :, pl.ds(0, HR)]
        dst = held.at[pl.ds(0, per_dev), :, pl.ds(HR + rows, HR)]
        return copy(src, dst, own_slot + 1, own_slot + 1, {"rows": line - 1})

    def has(p):
        return tm + p // per_dev < tm_count

    def spread(p):
        @pl.when(has(p) & (line + 1 < line_count))
        def _():
            down(p).start()

        @pl.when(has(p) & (line >= 1))
        def _():
            up(p).start()

    def sends_near(k):
        return (tm >= 1) & (odd if k < far else (tm >= 0))

    for k in range(far):

        @pl.when(tm >= 2)
        def _():
            distant(k).start()

    for k in list(range(far, per_dev)) + list(range(far)):

        @pl.when(sends_near(k))
        def _():
            near(k).start()

    @pl.when(line + 1 < line_count)
    def _():
        own_down().start()

    @pl.when(line >= 1)
    def _():
        own_up().start()

    ext_rows, tiles = held.shape[2], held.shape[3]
    blocks = tiles * LANES // BLOCK
    depth = wide.shape[1]

    def outer(a):
        return jnp.where(looks[0, a] >= HR, 1.0, 0.0).astype(jnp.float32)

    def place(p, r, get):
        parts = [get(part).astype(jnp.float32) for part in range(2)]
        outside = line == 0 if r < HR else line == line_count - 1 if r >= HR + rows else None
        if outside is not None:
            parts = [jnp.where(outside, 0.0, part) for part in parts]
        planes[p, 0, r] = parts[0]
        planes[p, 1, r] = parts[1]
        power[p, r] = parts[0] * parts[0] + parts[1] * parts[1]

    def row_window(get, field, edge_weight):
        for h in range(0, tiles, 8):
            v = get(h)
            pairs = [v[r] + v[r + 1] for r in range(1, rows + 2)]
            for r in range(rows):
                total_row = pairs[r] + v[r + 3] + (v[r] + v[r + 4]) * edge_weight
                sums[field, pl.ds(h * rows + r, 8, stride=rows), :] = total_row

    def box(a, count):
        for t in range(tiles):
            m, side = (t + 1) // 2, (t + 1) % 2
            for f in range(0, count, 2):
                pieces = [
                    sums[g, t * rows : (t + 1) * rows, :] for g in range(f, min(f + 2, count))
                ]
                piece = jnp.concatenate(pieces, 0).astype(jnp.bfloat16)
                at = slice(f * rows, f * rows + len(pieces) * rows)
                wide[m, at, side * LANES : (side + 1) * LANES] = piece
        lead = wide[0:blocks].reshape(blocks * depth, BLOCK)
        tail = wide[1 : blocks + 1].reshape(blocks * depth, BLOCK)
        result = jnp.dot(lead, bands[a, 0], preferred_element_type=jnp.float32)
        result = result + jnp.dot(tail, bands[a, 1], preferred_element_type=jnp.float32)
        return result.reshape(blocks, depth, BLOCK)

    def slot(a, p):
        weight = outer(a)

        def row(q, part, r, h):
            return planes[q, part, r, h : h + 8, :]

        def real_part(h):
            return [
                row(a, 0, r, h) * row(p, 0, r, h) + row(a, 1, r, h) * row(p, 1, r, h)
                for r in range(ext_rows)
            ]

        def imag_part(h):
            return [
                row(a, 1, r, h) * row(p, 0, r, h) - row(a, 0, r, h) * row(p, 1, r, h)
                for r in range(ext_rows)
            ]

        def partner_power(h):
            return [power[p, r, h : h + 8, :] for r in range(ext_rows)]

        row_window(real_part, 0, weight)
        row_window(imag_part, 1, weight)
        row_window(partner_power, 2, weight)
        boxed = box(a, 3)
        j = p - a - 1
        live = (j < counts[a]) & (tm * per_dev + p < acq_total)
        area = ((2 * looks[0, a] + 1) * (2 * looks[1, a] + 1)).astype(jnp.float32)
        scale = 1.0 / jnp.full((rows, BLOCK), area, jnp.float32)
        for n in range(blocks):
            own = own_box[a, n]
            real, imag, other = [boxed[n, f * rows : (f + 1) * rows, :] for f in range(3)]
            magnitude = jnp.sqrt(real * real + imag * imag)
            value = magnitude * lax.rsqrt(own * other + epsilon)
            where = slice(n * BLOCK, (n + 1) * BLOCK)
            ifg[a, j, 0, :, where] = jnp.where(live, real * scale, 0.0).astype(ifg.dtype)
            ifg[a, j, 1, :, where] = jnp.where(live, imag * scale, 0.0).astype(ifg.dtype)
            coh[a, j, :, where] = jnp.where(live, value, 0.0).astype(coh.dtype)

    def arrive(p):
        @pl.when(has(p))
        def _():
            near(p - per_dev).wait_recv()

        spread(p)

    def halo(p):
        @pl.when(has(p) & (line + 1 < line_count))
        def _():
            up(p).wait_recv()

        @pl.when(has(p) & (line >= 1))
        def _():
            down(p).wait_recv()

    zero = jnp.zeros((depth, LANES), wide.dtype)
    wide[0, :, :LANES] = zero
    wide[blocks, :, LANES:] = zero
    inner = lax.broadcasted_iota(jnp.int32, (BLOCK, BLOCK), 0)
    across = lax.broadcasted_iota(jnp.int32, (BLOCK, BLOCK), 1)

    @pl.loop(0, per_dev)
    def _(a):
        reach = looks[1, a]
        bands[a, 0] = jnp.where(jnp.abs(inner - LANES - across) <= reach, 1.0, 0.0).astype(
            jnp.bfloat16
        )
        bands[a, 1] = jnp.where(jnp.abs(inner + LANES - across) <= reach, 1.0, 0.0).astype(
            jnp.bfloat16
        )
        for r in range(rows):
            place(a, HR + r, lambda part: x[a, part, r])

    @pl.when(line >= 1)
    def _():
        own_down().wait_recv()

    @pl.when(line + 1 < line_count)
    def _():
        own_up().wait_recv()

    @pl.loop(0, per_dev)
    def _(a):
        for r in list(range(HR)) + list(range(HR + rows, ext_rows)):
            place(a, r, lambda part: held[a, part, r])
        weight = outer(a)
        row_window(lambda h: [power[a, r, h : h + 8, :] for r in range(ext_rows)], 0, weight)
        own_box[a] = box(a, 1)[:, :rows, :]

    for k in range(far):
        p = 2 * per_dev + k

        @pl.when(has(p))
        def _():
            distant(k).wait_recv()

        @pl.when(has(p) & even)
        def _():
            onward(k).start()

        spread(p)

    @pl.loop(0, per_dev - 1)
    def _(a):
        @pl.loop(a + 1, per_dev)
        def _(p):
            slot(a, p)

    order = [2 * per_dev + k for k in range(far)]
    order += [per_dev + k for k in range(far, per_dev)] + [per_dev + k for k in range(far)]

    for i, p in enumerate(order):
        halo(p)
        for r in range(ext_rows):
            place(p, r, lambda part: held[p, part, r])

        @pl.loop(max(0, p - MAXP), per_dev)
        def _(a):
            slot(a, p)

        if i + 2 < len(order) and order[i + 2] < 2 * per_dev:
            arrive(order[i + 2])

    @pl.when(line >= 1)
    def _():
        own_up().wait_send()

    @pl.when(line + 1 < line_count)
    def _():
        own_down().wait_send()

    for p in range(per_dev, total):

        @pl.when(has(p) & (line + 1 < line_count))
        def _():
            down(p).wait_send()

        @pl.when(has(p) & (line >= 1))
        def _():
            up(p).wait_send()

    for k in range(far):

        @pl.when(tm >= 2)
        def _():
            distant(k).wait_send()

        @pl.when(has(2 * per_dev + k) & even)
        def _():
            onward(k).wait_send()

    for k in range(per_dev):

        @pl.when(sends_near(k))
        def _():
            near(k).wait_send()


def computed(x, counts, looks, acq_total):
    per_dev, parts, rows, tiles, lanes = x.shape
    total, ext_rows = per_dev + MAXP, rows + 2 * HR
    cols = tiles * lanes
    blocks = cols // BLOCK
    slots = 3 * total + MAXP
    smem, vmem = [pl.BlockSpec(memory_space=space) for space in (pltpu.SMEM, pltpu.VMEM)]
    return pl.pallas_call(
        functools.partial(kernel, acq_total),
        in_specs=[smem, smem, vmem],
        out_specs=[vmem, vmem],
        out_shape=[
            jax.ShapeDtypeStruct((per_dev, MAXP, 2, rows, cols), jnp.bfloat16),
            jax.ShapeDtypeStruct((per_dev, MAXP, rows, cols), jnp.bfloat16),
        ],
        scratch_shapes=[
            pltpu.VMEM((total, parts, ext_rows, tiles, lanes), x.dtype),
            pltpu.VMEM((total, parts, ext_rows, tiles, lanes), jnp.float32),
            pltpu.VMEM((total, ext_rows, tiles, lanes), jnp.float32),
            pltpu.VMEM((3, tiles * rows, lanes), jnp.float32),
            pltpu.VMEM((blocks + 1, 4 * rows, BLOCK), jnp.bfloat16),
            pltpu.VMEM((per_dev, 2, BLOCK, BLOCK), jnp.bfloat16),
            pltpu.VMEM((per_dev, blocks, rows, BLOCK), jnp.float32),
            pltpu.SemaphoreType.DMA((slots,)),
            pltpu.SemaphoreType.DMA((slots,)),
        ],
        compiler_params=pltpu.CompilerParams(
            collective_id=0, has_side_effects=True, vmem_limit_bytes=40 * 1024 * 1024
        ),
        name="insar_boxes",
    )(counts, looks, x)


def local(slc_stack, partner_count, look_sizes):
    tiled = slc_stack.reshape(slc_stack.shape[:-1] + (-1, LANES))
    acq_total = lax.axis_size("tm") * slc_stack.shape[0]
    return tuple(computed(tiled, partner_count, look_sizes.T, acq_total))


def solution(mesh):
    return jax.shard_map(
        local,
        mesh=mesh,
        in_specs=(P("tm", None, "rows", None), P("tm"), P("tm", None)),
        out_specs=(P("tm", None, None, "rows", None), P("tm", None, "rows", None)),
        check_vma=False,
    )
```

```python
import functools

import jax
import jax.numpy as jnp
from jax import lax
from jax.experimental import pallas as pl
from jax.experimental.pallas import tpu as pltpu
from jax.sharding import PartitionSpec as P

MAXP = 6
HR = 2
LANES = 128
BLOCK = 256

epsilon = 1e-06
MESH = pl.DeviceIdType.MESH


def kernel(
    acq_total, counts_in, looks_in, x, ifg, coh,
    held, planes, power, sums, wide, bands, own_box, counts, looks,
    send_sem, recv_sem, table_sem,
):
    tm, line = lax.axis_index("tm"), lax.axis_index("rows")
    tm_count, line_count = lax.axis_size("tm"), lax.axis_size("rows")
    per_dev, _, rows = x.shape[:3]
    total = held.shape[0]
    far = MAXP - per_dev
    even = lax.rem(tm, 2) == 0
    odd = lax.rem(tm, 2) == 1
    steps = [
        (tm >= 1, {"tm": tm - 1}),
        (tm >= 2, {"tm": tm - 2}),
        (tm + 1 < tm_count, {"tm": tm + 1}),
        (tm + 2 < tm_count, {"tm": tm + 2}),
        (line >= 1, {"rows": line - 1}),
        (line + 1 < line_count, {"rows": line + 1}),
    ]
    tables = [
        pltpu.make_async_copy(counts_in, counts, table_sem.at[0]),
        pltpu.make_async_copy(looks_in, looks, table_sem.at[1]),
    ]
    for table in tables:
        table.start()
    barrier = pltpu.get_barrier_semaphore()
    for there, device in steps:

        @pl.when(there)
        def _():
            pl.semaphore_signal(barrier, inc=1, device_id=device, device_id_type=MESH)

    pl.semaphore_wait(barrier, sum(jnp.where(there, 1, 0) for there, _ in steps))

    body = pl.ds(HR, rows)
    forward_slot = 3 * total
    own_slot = 3 * total + far

    def copy(src, dst, send, recv, device):
        return pltpu.make_async_remote_copy(
            src_ref=src,
            dst_ref=dst,
            send_sem=send_sem.at[send],
            recv_sem=recv_sem.at[recv],
            device_id=device,
            device_id_type=MESH,
        )

    def near(k):
        spot = per_dev + k
        return copy(x.at[k], held.at[spot, :, body], spot, spot, {"tm": tm - 1})

    def distant(k):
        spot = 2 * per_dev + k
        return copy(x.at[k], held.at[spot, :, body], spot, spot, {"tm": tm - 2})

    def onward(k):
        spot = per_dev + k
        src = held.at[2 * per_dev + k, :, body]
        return copy(src, held.at[spot, :, body], forward_slot + k, spot, {"tm": tm + 1})

    def down(p):
        src = held.at[p, :, pl.ds(rows, HR)]
        slot = total + p
        return copy(src, held.at[p, :, pl.ds(0, HR)], slot, slot, {"rows": line + 1})

    def up(p):
        src = held.at[p, :, pl.ds(HR, HR)]
        slot = 2 * total + p
        return copy(src, held.at[p, :, pl.ds(HR + rows, HR)], slot, slot, {"rows": line - 1})

    def own_down():
        src = x.at[:, :, pl.ds(rows - HR, HR)]
        dst = held.at[pl.ds(0, per_dev), :, pl.ds(0, HR)]
        return copy(src, dst, own_slot, own_slot, {"rows": line + 1})

    def own_up():
        src = x.at[:, :, pl.ds(0, HR)]
        dst = held.at[pl.ds(0, per_dev), :, pl.ds(HR + rows, HR)]
        return copy(src, dst, own_slot + 1, own_slot + 1, {"rows": line - 1})

    def has(p):
        return tm + p // per_dev < tm_count

    def spread(p):
        @pl.when(has(p) & (line + 1 < line_count))
        def _():
            down(p).start()

        @pl.when(has(p) & (line >= 1))
        def _():
            up(p).start()

    def sends_near(k):
        return (tm >= 1) & (odd if k < far else (tm >= 0))

    for k in range(far):

        @pl.when(tm >= 2)
        def _():
            distant(k).start()

    for k in list(range(far, per_dev)) + list(range(far)):

        @pl.when(sends_near(k))
        def _():
            near(k).start()

    @pl.when(line + 1 < line_count)
    def _():
        own_down().start()

    @pl.when(line >= 1)
    def _():
        own_up().start()

    ext_rows, tiles = held.shape[2], held.shape[3]
    blocks = tiles * LANES // BLOCK
    depth = wide.shape[1]

    def outer(a):
        return jnp.where(looks[0, a] >= HR, 1.0, 0.0).astype(jnp.float32)

    def place(p, r, get):
        parts = [get(part).astype(jnp.float32) for part in range(2)]
        outside = line == 0 if r < HR else line == line_count - 1 if r >= HR + rows else None
        if outside is not None:
            parts = [jnp.where(outside, 0.0, part) for part in parts]
        planes[p, 0, r] = parts[0]
        planes[p, 1, r] = parts[1]
        power[p, r] = parts[0] * parts[0] + parts[1] * parts[1]

    def row_window(get, field, edge_weight):
        for h in range(0, tiles, 8):
            v = get(h)
            pairs = [v[r] + v[r + 1] for r in range(1, rows + 2)]
            for r in range(rows):
                total_row = pairs[r] + v[r + 3] + (v[r] + v[r + 4]) * edge_weight
                sums[field, pl.ds(h * rows + r, 8, stride=rows), :] = total_row

    def box(a, count):
        for t in range(tiles):
            m, side = (t + 1) // 2, (t + 1) % 2
            for f in range(0, count, 2):
                pieces = [
                    sums[g, t * rows : (t + 1) * rows, :] for g in range(f, min(f + 2, count))
                ]
                piece = jnp.concatenate(pieces, 0).astype(jnp.bfloat16)
                at = slice(f * rows, f * rows + len(pieces) * rows)
                wide[m, at, side * LANES : (side + 1) * LANES] = piece
        lead = wide[0:blocks].reshape(blocks * depth, BLOCK)
        tail = wide[1 : blocks + 1].reshape(blocks * depth, BLOCK)
        result = jnp.dot(lead, bands[a, 0], preferred_element_type=jnp.float32)
        result = result + jnp.dot(tail, bands[a, 1], preferred_element_type=jnp.float32)
        return result.reshape(blocks, depth, BLOCK)

    def slot(a, p):
        weight = outer(a)

        def row(q, part, r, h):
            return planes[q, part, r, h : h + 8, :]

        def real_part(h):
            return [
                row(a, 0, r, h) * row(p, 0, r, h) + row(a, 1, r, h) * row(p, 1, r, h)
                for r in range(ext_rows)
            ]

        def imag_part(h):
            return [
                row(a, 1, r, h) * row(p, 0, r, h) - row(a, 0, r, h) * row(p, 1, r, h)
                for r in range(ext_rows)
            ]

        def partner_power(h):
            return [power[p, r, h : h + 8, :] for r in range(ext_rows)]

        row_window(real_part, 0, weight)
        row_window(imag_part, 1, weight)
        row_window(partner_power, 2, weight)
        boxed = box(a, 3)
        j = p - a - 1
        live = (j < counts[a]) & (tm * per_dev + p < acq_total)
        area = ((2 * looks[0, a] + 1) * (2 * looks[1, a] + 1)).astype(jnp.float32)
        scale = 1.0 / jnp.full((rows, BLOCK), area, jnp.float32)
        for n in range(blocks):
            own = own_box[a, n]
            real, imag, other = [boxed[n, f * rows : (f + 1) * rows, :] for f in range(3)]
            magnitude = jnp.sqrt(real * real + imag * imag)
            value = magnitude * lax.rsqrt(own * other + epsilon)
            where = slice(n * BLOCK, (n + 1) * BLOCK)
            ifg[a, j, 0, :, where] = jnp.where(live, real * scale, 0.0).astype(ifg.dtype)
            ifg[a, j, 1, :, where] = jnp.where(live, imag * scale, 0.0).astype(ifg.dtype)
            coh[a, j, :, where] = jnp.where(live, value, 0.0).astype(coh.dtype)

    def arrive(p):
        @pl.when(has(p))
        def _():
            near(p - per_dev).wait_recv()

        spread(p)

    def halo(p):
        @pl.when(has(p) & (line + 1 < line_count))
        def _():
            up(p).wait_recv()

        @pl.when(has(p) & (line >= 1))
        def _():
            down(p).wait_recv()

    zero = jnp.zeros((depth, LANES), wide.dtype)
    wide[0, :, :LANES] = zero
    wide[blocks, :, LANES:] = zero
    inner = lax.broadcasted_iota(jnp.int32, (BLOCK, BLOCK), 0)
    across = lax.broadcasted_iota(jnp.int32, (BLOCK, BLOCK), 1)

    for table in tables:
        table.wait()

    @pl.loop(0, per_dev)
    def _(a):
        reach = looks[1, a]
        bands[a, 0] = jnp.where(jnp.abs(inner - LANES - across) <= reach, 1.0, 0.0).astype(
            jnp.bfloat16
        )
        bands[a, 1] = jnp.where(jnp.abs(inner + LANES - across) <= reach, 1.0, 0.0).astype(
            jnp.bfloat16
        )
        for r in range(rows):
            place(a, HR + r, lambda part: x[a, part, r])

    @pl.when(line >= 1)
    def _():
        own_down().wait_recv()

    @pl.when(line + 1 < line_count)
    def _():
        own_up().wait_recv()

    @pl.loop(0, per_dev)
    def _(a):
        for r in list(range(HR)) + list(range(HR + rows, ext_rows)):
            place(a, r, lambda part: held[a, part, r])
        weight = outer(a)
        row_window(lambda h: [power[a, r, h : h + 8, :] for r in range(ext_rows)], 0, weight)
        own_box[a] = box(a, 1)[:, :rows, :]

    for k in range(far):
        p = 2 * per_dev + k

        @pl.when(has(p))
        def _():
            distant(k).wait_recv()

        @pl.when(has(p) & even)
        def _():
            onward(k).start()

        spread(p)

    @pl.loop(0, per_dev - 1)
    def _(a):
        @pl.loop(a + 1, per_dev)
        def _(p):
            slot(a, p)

    order = [2 * per_dev + k for k in range(far)]
    order += [per_dev + k for k in range(far, per_dev)] + [per_dev + k for k in range(far)]

    for i, p in enumerate(order):
        halo(p)
        for r in range(ext_rows):
            place(p, r, lambda part: held[p, part, r])

        @pl.loop(max(0, p - MAXP), per_dev)
        def _(a):
            slot(a, p)

        if i + 2 < len(order) and order[i + 2] < 2 * per_dev:
            arrive(order[i + 2])

    @pl.when(line >= 1)
    def _():
        own_up().wait_send()

    @pl.when(line + 1 < line_count)
    def _():
        own_down().wait_send()

    for p in range(per_dev, total):

        @pl.when(has(p) & (line + 1 < line_count))
        def _():
            down(p).wait_send()

        @pl.when(has(p) & (line >= 1))
        def _():
            up(p).wait_send()

    for k in range(far):

        @pl.when(tm >= 2)
        def _():
            distant(k).wait_send()

        @pl.when(has(2 * per_dev + k) & even)
        def _():
            onward(k).wait_send()

    for k in range(per_dev):

        @pl.when(sends_near(k))
        def _():
            near(k).wait_send()


def computed(x, counts, looks, acq_total):
    per_dev, parts, rows, tiles, lanes = x.shape
    total, ext_rows = per_dev + MAXP, rows + 2 * HR
    cols = tiles * lanes
    blocks = cols // BLOCK
    slots = 3 * total + MAXP
    hbm, vmem = [pl.BlockSpec(memory_space=space) for space in (pl.ANY, pltpu.VMEM)]
    return pl.pallas_call(
        functools.partial(kernel, acq_total),
        in_specs=[hbm, hbm, vmem],
        out_specs=[vmem, vmem],
        out_shape=[
            jax.ShapeDtypeStruct((per_dev, MAXP, 2, rows, cols), jnp.bfloat16),
            jax.ShapeDtypeStruct((per_dev, MAXP, rows, cols), jnp.bfloat16),
        ],
        scratch_shapes=[
            pltpu.VMEM((total, parts, ext_rows, tiles, lanes), x.dtype),
            pltpu.VMEM((total, parts, ext_rows, tiles, lanes), jnp.float32),
            pltpu.VMEM((total, ext_rows, tiles, lanes), jnp.float32),
            pltpu.VMEM((3, tiles * rows, lanes), jnp.float32),
            pltpu.VMEM((blocks + 1, 4 * rows, BLOCK), jnp.bfloat16),
            pltpu.VMEM((per_dev, 2, BLOCK, BLOCK), jnp.bfloat16),
            pltpu.VMEM((per_dev, blocks, rows, BLOCK), jnp.float32),
            pltpu.SMEM((per_dev,), jnp.int32),
            pltpu.SMEM((2, per_dev), jnp.int32),
            pltpu.SemaphoreType.DMA((slots,)),
            pltpu.SemaphoreType.DMA((slots,)),
            pltpu.SemaphoreType.DMA((2,)),
        ],
        compiler_params=pltpu.CompilerParams(
            collective_id=0, has_side_effects=True, vmem_limit_bytes=40 * 1024 * 1024
        ),
        name="insar_boxes",
    )(counts, looks, x)


def local(slc_stack, partner_count, look_sizes):
    tiled = slc_stack.reshape(slc_stack.shape[:-1] + (-1, LANES))
    acq_total = lax.axis_size("tm") * slc_stack.shape[0]
    return tuple(computed(tiled, partner_count, look_sizes.T, acq_total))


def solution(mesh):
    return jax.shard_map(
        local,
        mesh=mesh,
        in_specs=(P("tm", None, "rows", None), P("tm"), P("tm", None)),
        out_specs=(P("tm", None, None, "rows", None), P("tm", None, "rows", None)),
        check_vma=False,
    )
```

```python
import functools

import jax
import jax.numpy as jnp
from jax import lax
from jax.experimental import pallas as pl
from jax.experimental.pallas import tpu as pltpu
from jax.sharding import PartitionSpec as P

MAXP = 6
HR = 2
LANES = 128
BLOCK = 256

epsilon = 1e-06
MESH = pl.DeviceIdType.MESH


def kernel(
    acq_total, counts_in, looks_in, x, ifg, coh,
    held, planes, power, sums, wide, bands, own_box, counts, looks,
    send_sem, recv_sem, table_sem,
):
    tm, line = lax.axis_index("tm"), lax.axis_index("rows")
    tm_count, line_count = lax.axis_size("tm"), lax.axis_size("rows")
    per_dev, _, rows = x.shape[:3]
    total = held.shape[0]
    far = MAXP - per_dev
    even = lax.rem(tm, 2) == 0
    odd = lax.rem(tm, 2) == 1
    steps = [
        (tm >= 1, {"tm": tm - 1}),
        (tm >= 2, {"tm": tm - 2}),
        (tm + 1 < tm_count, {"tm": tm + 1}),
        (tm + 2 < tm_count, {"tm": tm + 2}),
        (line >= 1, {"rows": line - 1}),
        (line + 1 < line_count, {"rows": line + 1}),
    ]
    tables = [
        pltpu.make_async_copy(counts_in, counts, table_sem.at[0]),
        pltpu.make_async_copy(looks_in, looks, table_sem.at[1]),
    ]
    for table in tables:
        table.start()
    barrier = pltpu.get_barrier_semaphore()
    for there, device in steps:

        @pl.when(there)
        def _():
            pl.semaphore_signal(barrier, inc=1, device_id=device, device_id_type=MESH)

    pl.semaphore_wait(barrier, sum(jnp.where(there, 1, 0) for there, _ in steps))

    near_dev, far_dev, next_dev = {"tm": tm - 1}, {"tm": tm - 2}, {"tm": tm + 1}
    starts = [per_dev, per_dev + far, 2 * per_dev]
    sizes = [far, per_dev - far, far]
    sides = [(0, HR), (rows - HR, rows)]
    mid_slot = 6
    down_slot = mid_slot + MAXP
    up_slot = down_slot + 3
    own_slot = up_slot + 3
    onward_slot = own_slot + 2

    def copy(src, dst, send, recv, device):
        return pltpu.make_async_remote_copy(
            src_ref=src,
            dst_ref=dst,
            send_sem=send_sem.at[send],
            recv_sem=recv_sem.at[recv],
            device_id=device,
            device_id_type=MESH,
        )

    def span(g, low, high):
        return held.at[pl.ds(starts[g], sizes[g]), :, pl.ds(HR + low, high - low)]

    def edge(g, side, device):
        low, high = sides[side]
        src = x.at[pl.ds(starts[g] % per_dev, sizes[g]), :, pl.ds(low, high - low)]
        return copy(src, span(g, low, high), 2 * g + side, 2 * g + side, device)

    def middle(p, device):
        src = x.at[p % per_dev, :, pl.ds(HR, rows - 2 * HR)]
        dst = held.at[p, :, pl.ds(2 * HR, rows - 2 * HR)]
        slot_at = mid_slot + p - per_dev
        return copy(src, dst, slot_at, slot_at, device)

    def onward_edge(side):
        low, high = sides[side]
        return copy(span(2, low, high), span(0, low, high), onward_slot + side, side, next_dev)

    def onward_middle(k):
        src = held.at[2 * per_dev + k, :, pl.ds(2 * HR, rows - 2 * HR)]
        dst = held.at[per_dev + k, :, pl.ds(2 * HR, rows - 2 * HR)]
        return copy(src, dst, onward_slot + 2 + k, mid_slot + k, next_dev)

    def down(g):
        src, dst = span(g, rows - HR, rows), span(g, -HR, 0)
        return copy(src, dst, down_slot + g, down_slot + g, {"rows": line + 1})

    def up(g):
        src, dst = span(g, 0, HR), span(g, rows, rows + HR)
        return copy(src, dst, up_slot + g, up_slot + g, {"rows": line - 1})

    def own_down():
        src = x.at[:, :, pl.ds(rows - HR, HR)]
        dst = held.at[pl.ds(0, per_dev), :, pl.ds(0, HR)]
        return copy(src, dst, own_slot, own_slot, {"rows": line + 1})

    def own_up():
        src = x.at[:, :, pl.ds(0, HR)]
        dst = held.at[pl.ds(0, per_dev), :, pl.ds(HR + rows, HR)]
        return copy(src, dst, own_slot + 1, own_slot + 1, {"rows": line - 1})

    below, above = line + 1 < line_count, line >= 1
    has = [tm + 1 < tm_count, tm + 1 < tm_count, tm + 2 < tm_count]
    passes = even & has[2]
    sends = [odd, tm >= 1, tm >= 2]
    to = [near_dev, near_dev, far_dev]

    @pl.when(below)
    def _():
        own_down().start()

    @pl.when(above)
    def _():
        own_up().start()

    for g in (2, 1, 0):

        @pl.when(sends[g])
        def _():
            for side in range(2):
                edge(g, side, to[g]).start()

    for g in (2, 1, 0):

        @pl.when(sends[g])
        def _():
            for k in range(sizes[g]):
                middle(starts[g] + k, to[g]).start()

    ext_rows, tiles = held.shape[2], held.shape[3]
    blocks = tiles * LANES // BLOCK
    depth = wide.shape[1]

    def outer(a):
        return jnp.where(looks[0, a] >= HR, 1.0, 0.0).astype(jnp.float32)

    def place(p, r, get):
        parts = [get(part).astype(jnp.float32) for part in range(2)]
        outside = line == 0 if r < HR else line == line_count - 1 if r >= HR + rows else None
        if outside is not None:
            parts = [jnp.where(outside, 0.0, part) for part in parts]
        planes[p, 0, r] = parts[0]
        planes[p, 1, r] = parts[1]
        power[p, r] = parts[0] * parts[0] + parts[1] * parts[1]

    def row_window(get, field, edge_weight):
        for h in range(0, tiles, 8):
            v = get(h)
            pairs = [v[r] + v[r + 1] for r in range(1, rows + 2)]
            for r in range(rows):
                total_row = pairs[r] + v[r + 3] + (v[r] + v[r + 4]) * edge_weight
                sums[field, pl.ds(h * rows + r, 8, stride=rows), :] = total_row

    def box(a, count):
        for t in range(tiles):
            m, side = (t + 1) // 2, (t + 1) % 2
            for f in range(0, count, 2):
                pieces = [
                    sums[g, t * rows : (t + 1) * rows, :] for g in range(f, min(f + 2, count))
                ]
                piece = jnp.concatenate(pieces, 0).astype(jnp.bfloat16)
                at = slice(f * rows, f * rows + len(pieces) * rows)
                wide[m, at, side * LANES : (side + 1) * LANES] = piece
        lead = wide[0:blocks].reshape(blocks * depth, BLOCK)
        tail = wide[1 : blocks + 1].reshape(blocks * depth, BLOCK)
        result = jnp.dot(lead, bands[a, 0], preferred_element_type=jnp.float32)
        result = result + jnp.dot(tail, bands[a, 1], preferred_element_type=jnp.float32)
        return result.reshape(blocks, depth, BLOCK)

    def slot(a, p):
        weight = outer(a)

        def row(q, part, r, h):
            return planes[q, part, r, h : h + 8, :]

        def real_part(h):
            return [
                row(a, 0, r, h) * row(p, 0, r, h) + row(a, 1, r, h) * row(p, 1, r, h)
                for r in range(ext_rows)
            ]

        def imag_part(h):
            return [
                row(a, 1, r, h) * row(p, 0, r, h) - row(a, 0, r, h) * row(p, 1, r, h)
                for r in range(ext_rows)
            ]

        def partner_power(h):
            return [power[p, r, h : h + 8, :] for r in range(ext_rows)]

        row_window(real_part, 0, weight)
        row_window(imag_part, 1, weight)
        row_window(partner_power, 2, weight)
        boxed = box(a, 3)
        j = p - a - 1
        live = (j < counts[a]) & (tm * per_dev + p < acq_total)
        area = ((2 * looks[0, a] + 1) * (2 * looks[1, a] + 1)).astype(jnp.float32)
        scale = 1.0 / jnp.full((rows, BLOCK), area, jnp.float32)
        for n in range(blocks):
            own = own_box[a, n]
            real, imag, other = [boxed[n, f * rows : (f + 1) * rows, :] for f in range(3)]
            magnitude = jnp.sqrt(real * real + imag * imag)
            value = magnitude * lax.rsqrt(own * other + epsilon)
            where = slice(n * BLOCK, (n + 1) * BLOCK)
            ifg[a, j, 0, :, where] = jnp.where(live, real * scale, 0.0).astype(ifg.dtype)
            ifg[a, j, 1, :, where] = jnp.where(live, imag * scale, 0.0).astype(ifg.dtype)
            coh[a, j, :, where] = jnp.where(live, value, 0.0).astype(coh.dtype)

    def relay(g):
        @pl.when(has[g])
        def _():
            for side in range(2):
                edge(g, side, to[g]).wait_recv()

        if g == 2:

            @pl.when(passes)
            def _():
                for side in range(2):
                    onward_edge(side).start()

        @pl.when(has[g] & below)
        def _():
            down(g).start()

        @pl.when(has[g] & above)
        def _():
            up(g).start()

    def halo(g):
        @pl.when(has[g] & below)
        def _():
            up(g).wait_recv()

        @pl.when(has[g] & above)
        def _():
            down(g).wait_recv()

    zero = jnp.zeros((depth, LANES), wide.dtype)
    wide[0, :, :LANES] = zero
    wide[blocks, :, LANES:] = zero
    inner = lax.broadcasted_iota(jnp.int32, (BLOCK, BLOCK), 0)
    across = lax.broadcasted_iota(jnp.int32, (BLOCK, BLOCK), 1)

    for table in tables:
        table.wait()

    @pl.loop(0, per_dev)
    def _(a):
        reach = looks[1, a]
        bands[a, 0] = jnp.where(jnp.abs(inner - LANES - across) <= reach, 1.0, 0.0).astype(
            jnp.bfloat16
        )
        bands[a, 1] = jnp.where(jnp.abs(inner + LANES - across) <= reach, 1.0, 0.0).astype(
            jnp.bfloat16
        )
        for r in range(rows):
            place(a, HR + r, lambda part: x[a, part, r])

    relay(2)
    relay(1)

    @pl.when(line >= 1)
    def _():
        own_down().wait_recv()

    @pl.when(line + 1 < line_count)
    def _():
        own_up().wait_recv()

    @pl.loop(0, per_dev)
    def _(a):
        for r in list(range(HR)) + list(range(HR + rows, ext_rows)):
            place(a, r, lambda part: held[a, part, r])
        weight = outer(a)
        row_window(lambda h: [power[a, r, h : h + 8, :] for r in range(ext_rows)], 0, weight)
        own_box[a] = box(a, 1)[:, :rows, :]

    @pl.when(has[2])
    def _():
        for k in range(far):
            middle(2 * per_dev + k, far_dev).wait_recv()

    @pl.when(passes)
    def _():
        for k in range(far):
            onward_middle(k).start()

    relay(0)

    @pl.loop(0, per_dev - 1)
    def _(a):
        @pl.loop(a + 1, per_dev)
        def _(p):
            slot(a, p)

    order = [2 * per_dev + k for k in range(far)]
    order += [per_dev + k for k in range(far, per_dev)] + [per_dev + k for k in range(far)]

    for p in order:
        g = 2 if p >= starts[2] else 1 if p >= starts[1] else 0
        if g < 2:

            @pl.when(has[g])
            def _():
                middle(p, to[g]).wait_recv()

        if p == starts[g]:
            halo(g)

        for r in range(ext_rows):
            place(p, r, lambda part: held[p, part, r])

        @pl.loop(max(0, p - MAXP), per_dev)
        def _(a):
            slot(a, p)

    @pl.when(above)
    def _():
        own_up().wait_send()

    @pl.when(below)
    def _():
        own_down().wait_send()

    for g in range(3):

        @pl.when(has[g] & below)
        def _():
            down(g).wait_send()

        @pl.when(has[g] & above)
        def _():
            up(g).wait_send()

        @pl.when(sends[g])
        def _():
            for side in range(2):
                edge(g, side, to[g]).wait_send()
            for k in range(sizes[g]):
                middle(starts[g] + k, to[g]).wait_send()

    @pl.when(passes)
    def _():
        for side in range(2):
            onward_edge(side).wait_send()
        for k in range(far):
            onward_middle(k).wait_send()


def computed(x, counts, looks, acq_total):
    per_dev, parts, rows, tiles, lanes = x.shape
    total, ext_rows = per_dev + MAXP, rows + 2 * HR
    cols = tiles * lanes
    blocks = cols // BLOCK
    slots = 16 + 2 * MAXP
    hbm, vmem = [pl.BlockSpec(memory_space=space) for space in (pltpu.HBM, pltpu.VMEM)]
    return pl.pallas_call(
        functools.partial(kernel, acq_total),
        in_specs=[hbm, hbm, vmem],
        out_specs=[vmem, vmem],
        out_shape=[
            jax.ShapeDtypeStruct((per_dev, MAXP, 2, rows, cols), jnp.bfloat16),
            jax.ShapeDtypeStruct((per_dev, MAXP, rows, cols), jnp.bfloat16),
        ],
        scratch_shapes=[
            pltpu.VMEM((total, parts, ext_rows, tiles, lanes), x.dtype),
            pltpu.VMEM((total, parts, ext_rows, tiles, lanes), jnp.float32),
            pltpu.VMEM((total, ext_rows, tiles, lanes), jnp.float32),
            pltpu.VMEM((3, tiles * rows, lanes), jnp.float32),
            pltpu.VMEM((blocks + 1, 4 * rows, BLOCK), jnp.bfloat16),
            pltpu.VMEM((per_dev, 2, BLOCK, BLOCK), jnp.bfloat16),
            pltpu.VMEM((per_dev, blocks, rows, BLOCK), jnp.float32),
            pltpu.SMEM((per_dev,), jnp.int32),
            pltpu.SMEM((2, per_dev), jnp.int32),
            pltpu.SemaphoreType.DMA((slots,)),
            pltpu.SemaphoreType.DMA((slots,)),
            pltpu.SemaphoreType.DMA((2,)),
        ],
        compiler_params=pltpu.CompilerParams(
            collective_id=0, has_side_effects=True, vmem_limit_bytes=40 * 1024 * 1024
        ),
        name="insar_boxes",
    )(counts, looks, x)


def local(slc_stack, partner_count, look_sizes):
    tiled = slc_stack.reshape(slc_stack.shape[:-1] + (-1, LANES))
    acq_total = lax.axis_size("tm") * slc_stack.shape[0]
    return tuple(computed(tiled, partner_count, look_sizes.T, acq_total))


def solution(mesh):
    return jax.shard_map(
        local,
        mesh=mesh,
        in_specs=(P("tm", None, "rows", None), P("tm"), P("tm", None)),
        out_specs=(P("tm", None, None, "rows", None), P("tm", None, "rows", None)),
        check_vma=False,
    )
```

```python
import functools

import jax
import jax.numpy as jnp
from jax import lax
from jax.experimental import pallas as pl
from jax.experimental.pallas import tpu as pltpu
from jax.sharding import PartitionSpec as P

MAXP = 6
HR = 2
LANES = 128
BLOCK = 256

epsilon = 1e-06
MESH = pl.DeviceIdType.MESH


def kernel(
    acq_total, counts_in, looks_in, x, ifg, coh,
    held, planes, power, sums, wide, bands, own_box, counts, looks,
    send_sem, recv_sem, table_sem,
):
    tm, line = lax.axis_index("tm"), lax.axis_index("rows")
    tm_count, line_count = lax.axis_size("tm"), lax.axis_size("rows")
    per_dev, _, rows = x.shape[:3]
    total = held.shape[0]
    far = MAXP - per_dev
    even = lax.rem(tm, 2) == 0
    odd = lax.rem(tm, 2) == 1
    steps = [
        (tm >= 1, {"tm": tm - 1}),
        (tm >= 2, {"tm": tm - 2}),
        (tm + 1 < tm_count, {"tm": tm + 1}),
        (tm + 2 < tm_count, {"tm": tm + 2}),
        (line >= 1, {"rows": line - 1}),
        (line + 1 < line_count, {"rows": line + 1}),
    ]
    tables = [
        pltpu.make_async_copy(counts_in, counts, table_sem.at[0]),
        pltpu.make_async_copy(looks_in, looks, table_sem.at[1]),
    ]
    for table in tables:
        table.start()
    barrier = pltpu.get_barrier_semaphore()
    for there, device in steps:

        @pl.when(there)
        def _():
            pl.semaphore_signal(barrier, inc=1, device_id=device, device_id_type=MESH)

    pl.semaphore_wait(barrier, sum(jnp.where(there, 1, 0) for there, _ in steps))

    near_dev, far_dev, next_dev = {"tm": tm - 1}, {"tm": tm - 2}, {"tm": tm + 1}
    starts = [per_dev, per_dev + far, 2 * per_dev]
    sizes = [far, per_dev - far, far]
    sides = [(0, HR), (rows - HR, rows)]
    mid_slot = 6
    down_slot = mid_slot + MAXP
    up_slot = down_slot + 3
    own_slot = up_slot + 3
    onward_slot = own_slot + 2

    def copy(src, dst, send, recv, device):
        return pltpu.make_async_remote_copy(
            src_ref=src,
            dst_ref=dst,
            send_sem=send_sem.at[send],
            recv_sem=recv_sem.at[recv],
            device_id=device,
            device_id_type=MESH,
        )

    def span(g, low, high):
        return held.at[pl.ds(starts[g], sizes[g]), :, pl.ds(HR + low, high - low)]

    def edge(g, side, device):
        low, high = sides[side]
        src = x.at[pl.ds(starts[g] % per_dev, sizes[g]), :, pl.ds(low, high - low)]
        return copy(src, span(g, low, high), 2 * g + side, 2 * g + side, device)

    def middle(p, device):
        src = x.at[p % per_dev, :, pl.ds(HR, rows - 2 * HR)]
        dst = held.at[p, :, pl.ds(2 * HR, rows - 2 * HR)]
        slot_at = mid_slot + p - per_dev
        return copy(src, dst, slot_at, slot_at, device)

    def onward_edge(side):
        low, high = sides[side]
        return copy(span(2, low, high), span(0, low, high), onward_slot + side, side, next_dev)

    def onward_middle(k):
        src = held.at[2 * per_dev + k, :, pl.ds(2 * HR, rows - 2 * HR)]
        dst = held.at[per_dev + k, :, pl.ds(2 * HR, rows - 2 * HR)]
        return copy(src, dst, onward_slot + 2 + k, mid_slot + k, next_dev)

    def down(g):
        src, dst = span(g, rows - HR, rows), span(g, -HR, 0)
        return copy(src, dst, down_slot + g, down_slot + g, {"rows": line + 1})

    def up(g):
        src, dst = span(g, 0, HR), span(g, rows, rows + HR)
        return copy(src, dst, up_slot + g, up_slot + g, {"rows": line - 1})

    def own_down():
        src = x.at[:, :, pl.ds(rows - HR, HR)]
        dst = held.at[pl.ds(0, per_dev), :, pl.ds(0, HR)]
        return copy(src, dst, own_slot, own_slot, {"rows": line + 1})

    def own_up():
        src = x.at[:, :, pl.ds(0, HR)]
        dst = held.at[pl.ds(0, per_dev), :, pl.ds(HR + rows, HR)]
        return copy(src, dst, own_slot + 1, own_slot + 1, {"rows": line - 1})

    below, above = line + 1 < line_count, line >= 1
    has = [tm + 1 < tm_count, tm + 1 < tm_count, tm + 2 < tm_count]
    passes = even & has[2]
    sends = [odd, tm >= 1, tm >= 2]
    to = [near_dev, near_dev, far_dev]

    @pl.when(below)
    def _():
        own_down().start()

    @pl.when(above)
    def _():
        own_up().start()

    for g in (2, 1, 0):

        @pl.when(sends[g])
        def _():
            for side in range(2):
                edge(g, side, to[g]).start()

    for g in (2, 1, 0):

        @pl.when(sends[g])
        def _():
            for k in range(sizes[g]):
                middle(starts[g] + k, to[g]).start()

    ext_rows, tiles = held.shape[2], held.shape[3]
    blocks = tiles * LANES // BLOCK
    depth = wide.shape[1]

    def outer(a):
        return jnp.where(looks[0, a] >= HR, 1.0, 0.0).astype(jnp.float32)

    def place(p, r, get):
        parts = [get(part).astype(jnp.float32) for part in range(2)]
        outside = line == 0 if r < HR else line == line_count - 1 if r >= HR + rows else None
        if outside is not None:
            parts = [jnp.where(outside, 0.0, part) for part in parts]
        planes[p, 0, r] = parts[0]
        planes[p, 1, r] = parts[1]
        power[p, r] = parts[0] * parts[0] + parts[1] * parts[1]

    def row_window(get, field, edge_weight):
        for h in range(0, tiles, 8):
            v = get(h)
            pairs = [v[r] + v[r + 1] for r in range(1, rows + 2)]
            for r in range(rows):
                total_row = pairs[r] + v[r + 3] + (v[r] + v[r + 4]) * edge_weight
                sums[field, pl.ds(h * rows + r, 8, stride=rows), :] = total_row

    def box(a, count):
        for t in range(tiles):
            m, side = (t + 1) // 2, (t + 1) % 2
            for f in range(0, count, 2):
                pieces = [
                    sums[g, t * rows : (t + 1) * rows, :] for g in range(f, min(f + 2, count))
                ]
                piece = jnp.concatenate(pieces, 0).astype(jnp.bfloat16)
                at = slice(f * rows, f * rows + len(pieces) * rows)
                wide[m, at, side * LANES : (side + 1) * LANES] = piece
        lead = wide[0:blocks].reshape(blocks * depth, BLOCK)
        tail = wide[1 : blocks + 1].reshape(blocks * depth, BLOCK)
        result = jnp.dot(lead, bands[a, 0], preferred_element_type=jnp.float32)
        result = result + jnp.dot(tail, bands[a, 1], preferred_element_type=jnp.float32)
        return result.reshape(blocks, depth, BLOCK)

    def slot(a, p):
        weight = outer(a)

        def row(q, part, r, h):
            return planes[q, part, r, h : h + 8, :]

        def real_part(h):
            return [
                row(a, 0, r, h) * row(p, 0, r, h) + row(a, 1, r, h) * row(p, 1, r, h)
                for r in range(ext_rows)
            ]

        def imag_part(h):
            return [
                row(a, 1, r, h) * row(p, 0, r, h) - row(a, 0, r, h) * row(p, 1, r, h)
                for r in range(ext_rows)
            ]

        def partner_power(h):
            return [power[p, r, h : h + 8, :] for r in range(ext_rows)]

        row_window(real_part, 0, weight)
        row_window(imag_part, 1, weight)
        row_window(partner_power, 2, weight)
        boxed = box(a, 3)
        j = p - a - 1
        live = (j < counts[a]) & (tm * per_dev + p < acq_total)
        area = ((2 * looks[0, a] + 1) * (2 * looks[1, a] + 1)).astype(jnp.float32)
        scale = 1.0 / jnp.full((rows, BLOCK), area, jnp.float32)
        for n in range(blocks):
            own = own_box[a, n]
            real, imag, other = [boxed[n, f * rows : (f + 1) * rows, :] for f in range(3)]
            magnitude = jnp.sqrt(real * real + imag * imag)
            value = magnitude * lax.rsqrt(own * other + epsilon)
            where = slice(n * BLOCK, (n + 1) * BLOCK)
            ifg[a, j, 0, :, where] = jnp.where(live, real * scale, 0.0).astype(ifg.dtype)
            ifg[a, j, 1, :, where] = jnp.where(live, imag * scale, 0.0).astype(ifg.dtype)
            coh[a, j, :, where] = jnp.where(live, value, 0.0).astype(coh.dtype)

    def relay(g):
        @pl.when(has[g])
        def _():
            for side in range(2):
                edge(g, side, to[g]).wait_recv()

        if g == 2:

            @pl.when(passes)
            def _():
                for side in range(2):
                    onward_edge(side).start()

        @pl.when(has[g] & below)
        def _():
            down(g).start()

        @pl.when(has[g] & above)
        def _():
            up(g).start()

    def halo(g):
        @pl.when(has[g] & below)
        def _():
            up(g).wait_recv()

        @pl.when(has[g] & above)
        def _():
            down(g).wait_recv()

    zero = jnp.zeros((depth, LANES), wide.dtype)
    wide[0, :, :LANES] = zero
    wide[blocks, :, LANES:] = zero
    inner = lax.broadcasted_iota(jnp.int32, (BLOCK, BLOCK), 0)
    across = lax.broadcasted_iota(jnp.int32, (BLOCK, BLOCK), 1)

    for table in tables:
        table.wait()

    @pl.loop(0, per_dev)
    def _(a):
        reach = looks[1, a]
        bands[a, 0] = jnp.where(jnp.abs(inner - LANES - across) <= reach, 1.0, 0.0).astype(
            jnp.bfloat16
        )
        bands[a, 1] = jnp.where(jnp.abs(inner + LANES - across) <= reach, 1.0, 0.0).astype(
            jnp.bfloat16
        )
        for r in range(rows):
            place(a, HR + r, lambda part: x[a, part, r])

    relay(2)
    relay(1)

    @pl.when(line >= 1)
    def _():
        own_down().wait_recv()

    @pl.when(line + 1 < line_count)
    def _():
        own_up().wait_recv()

    @pl.loop(0, per_dev)
    def _(a):
        for r in list(range(HR)) + list(range(HR + rows, ext_rows)):
            place(a, r, lambda part: held[a, part, r])
        weight = outer(a)
        row_window(lambda h: [power[a, r, h : h + 8, :] for r in range(ext_rows)], 0, weight)
        own_box[a] = box(a, 1)[:, :rows, :]

    @pl.when(has[2])
    def _():
        for k in range(far):
            middle(2 * per_dev + k, far_dev).wait_recv()

    @pl.when(passes)
    def _():
        for k in range(far):
            onward_middle(k).start()

    relay(0)

    @pl.loop(0, per_dev - 1)
    def _(a):
        @pl.loop(a + 1, per_dev)
        def _(p):
            slot(a, p)

    order = [2 * per_dev + k for k in range(far)]
    order += [per_dev + k for k in range(far, per_dev)] + [per_dev + k for k in range(far)]

    for p in order:
        g = 2 if p >= starts[2] else 1 if p >= starts[1] else 0
        if g < 2:

            @pl.when(has[g])
            def _():
                middle(p, to[g]).wait_recv()

        if p == starts[g]:
            halo(g)

        for r in range(ext_rows):
            place(p, r, lambda part: held[p, part, r])

        @pl.loop(max(0, p - MAXP), per_dev)
        def _(a):
            slot(a, p)

    @pl.when(above)
    def _():
        own_up().wait_send()

    @pl.when(below)
    def _():
        own_down().wait_send()

    for g in range(3):

        @pl.when(has[g] & below)
        def _():
            down(g).wait_send()

        @pl.when(has[g] & above)
        def _():
            up(g).wait_send()

        @pl.when(sends[g])
        def _():
            for side in range(2):
                edge(g, side, to[g]).wait_send()
            for k in range(sizes[g]):
                middle(starts[g] + k, to[g]).wait_send()

    @pl.when(passes)
    def _():
        for side in range(2):
            onward_edge(side).wait_send()
        for k in range(far):
            onward_middle(k).wait_send()


def computed(x, counts, looks, acq_total):
    per_dev, parts, rows, tiles, lanes = x.shape
    total, ext_rows = per_dev + MAXP, rows + 2 * HR
    cols = tiles * lanes
    blocks = cols // BLOCK
    slots = 16 + 2 * MAXP
    hbm, vmem = [pl.BlockSpec(memory_space=space) for space in (pltpu.HBM, pltpu.VMEM)]
    return pl.pallas_call(
        functools.partial(kernel, acq_total),
        in_specs=[hbm, hbm, vmem],
        out_specs=[vmem, vmem],
        out_shape=[
            jax.ShapeDtypeStruct((per_dev, MAXP, 2, rows, cols), jnp.bfloat16),
            jax.ShapeDtypeStruct((per_dev, MAXP, rows, cols), jnp.bfloat16),
        ],
        scratch_shapes=[
            pltpu.VMEM((total, parts, ext_rows, tiles, lanes), x.dtype),
            pltpu.VMEM((total, parts, ext_rows, tiles, lanes), jnp.float32),
            pltpu.VMEM((total, ext_rows, tiles, lanes), jnp.float32),
            pltpu.VMEM((3, tiles * rows, lanes), jnp.float32),
            pltpu.VMEM((blocks + 1, 4 * rows, BLOCK), jnp.bfloat16),
            pltpu.VMEM((per_dev, 2, BLOCK, BLOCK), jnp.bfloat16),
            pltpu.VMEM((per_dev, blocks, rows, BLOCK), jnp.float32),
            pltpu.SMEM((per_dev,), jnp.int32),
            pltpu.SMEM((2, per_dev), jnp.int32),
            pltpu.SemaphoreType.DMA((slots,)),
            pltpu.SemaphoreType.DMA((slots,)),
            pltpu.SemaphoreType.DMA((2,)),
        ],
        compiler_params=pltpu.CompilerParams(
            collective_id=0, has_side_effects=True, vmem_limit_bytes=40 * 1024 * 1024
        ),
        name="insar_boxes",
    )(*[pltpu.with_memory_space_constraint(table, pltpu.HBM) for table in (counts, looks)], x)


def local(slc_stack, partner_count, look_sizes):
    tiled = slc_stack.reshape(slc_stack.shape[:-1] + (-1, LANES))
    acq_total = lax.axis_size("tm") * slc_stack.shape[0]
    return tuple(computed(tiled, partner_count, look_sizes.T, acq_total))


def solution(mesh):
    return jax.shard_map(
        local,
        mesh=mesh,
        in_specs=(P("tm", None, "rows", None), P("tm"), P("tm", None)),
        out_specs=(P("tm", None, None, "rows", None), P("tm", None, "rows", None)),
        check_vma=False,
    )
```
